32 devices in a mesh: wide: 8 (over z, x), narrow: 4 (over y, core).
Axes of the slice: x: 2, y: 2, z: 4, core: 2. Of those that a mesh axis runs over, the one named last changes fastest.
Arguments:
- a_blocks: float32 [6144, 128, 128], P(('wide', 'narrow')), may hold values from -0.8 to 0.8
- row_map: int32 [6144, 128], P(('wide', 'narrow')), may hold values from 0 to 127
- col_map: int32 [6144, 128], P(('wide', 'narrow')), may hold values from 0 to 127
- target: int32 [6144], P(('wide', 'narrow')), may hold values from 0 to 839
- counts: int32 [8], P('wide'), may hold values from 1 to 8, as said below
- weights: int32 [64], P('wide'), may hold values from 1 to 999
Outputs:
- coarse: float32 [64, 128, 128], P('wide', 'narrow')
- work_offset: int32 [64], P('wide')
The draws below stay inside these ranges and needn't reach their ends.
Inputs may be any that keep to these rules, and one draw needn't show every extreme that they name: `counts`: every index of wide has at least one live slot and at most 8; some index has exactly 8; the last index has fewer than 8.
All inputs are finite; a program needn't handle non-finite values.
Results may differ from the reference program's by a relative error of at most 0.0003.
Values sent between devices are 32-bit elements; how exact they have to be, the bound alone decides.
No kernel may reach another device: no remote copies, remote signals or barrier semaphores. Data moves between devices by JAX's collectives and lax.ppermute only.
A program may use at most 128 MiB of HBM per device.

```python
import jax
import jax.numpy as jnp
from jax import lax

BS = 128
NB_DEV = 192
S_DEV = 8
BLOCKS = 6144
COARSE = 64
N_WIDE = 8
N_NARROW = 4


def draw_counts(key, part):
    first, second, third = jax.random.split(jax.random.fold_in(key, 17), 3)
    exponent = jax.random.randint(first, (N_WIDE,), 0, 4)
    ceiling = jnp.minimum(jnp.left_shift(1, exponent), S_DEV)
    positions = jnp.arange(N_WIDE)
    ceiling = jnp.where(positions == N_WIDE - 1, jnp.minimum(ceiling, S_DEV - 1), ceiling)
    values = 1 + jax.random.randint(second, (N_WIDE,), 0, 840) % ceiling
    chosen = jax.random.randint(third, (), 0, N_WIDE - 1)
    values = jnp.where(positions == chosen, S_DEV, values)
    return values.astype(jnp.int32)


def touch_ends(values, key, low, high):
    place = [jax.random.randint(jax.random.fold_in(key, axis), (), 0, length) for axis, length in enumerate(values.shape)]
    longest = values.shape.index(max(values.shape))
    next_to = place[:longest] + [(place[longest] + 1) % values.shape[longest]] + place[longest + 1:]
    return values.at[tuple(place)].set(low).at[tuple(next_to)].set(high)


def level_of(rng, dims, cuts, low, largest):
    level = 1.0
    for dim, parts in cuts:
        steps = jax.random.uniform(jax.random.fold_in(jax.random.fold_in(rng, 6), dim), (parts,), jnp.float32, low / len(cuts), largest / len(cuts))
        level = level * jnp.repeat(jnp.exp(steps), dims[dim] // parts).reshape((-1,) + (1,) * (len(dims) - 1 - dim))
    return level


def noise(rng, shape, width, reach, shards=(), held_as=jnp.bfloat16):
    values = jax.random.normal(rng, shape, jnp.float32) * width
    if len(shards) > 0:
        values = level_of(rng, shape, shards, -0.22, 0.18) * values
    return jnp.clip(values, min=-reach, max=reach).astype(held_as)


def setup_inputs(seed: int = 0) -> dict:
    key_list = jax.random.split(jax.random.key(seed), 7)
    a_blocks = noise(key_list[0], (BLOCKS, BS, BS), 0.1, 0.8, ((0, 32),), jnp.float32)
    row_map = touch_ends(jax.random.randint(key_list[1], (BLOCKS, BS), 0, BS), jax.random.fold_in(key_list[1], 1), 0, BS - 1).astype(jnp.int32)
    col_map = touch_ends(jax.random.randint(key_list[2], (BLOCKS, BS), 0, BS), jax.random.fold_in(key_list[2], 1), 0, BS - 1).astype(jnp.int32)
    target = touch_ends(jax.random.randint(key_list[3], (BLOCKS,), 0, 840), jax.random.fold_in(key_list[3], 1), 0, 839).astype(jnp.int32)
    counts = draw_counts(jax.random.fold_in(key_list[6], 71), 0)
    weights = touch_ends(jax.random.randint(key_list[5], (COARSE,), 1, 1000), jax.random.fold_in(key_list[5], 1), 1, 999).astype(jnp.int32)
    return dict(a_blocks=a_blocks, row_map=row_map, col_map=col_map, target=target, counts=counts, weights=weights)


def reference(a_blocks, row_map, col_map, target, counts, weights):
    per_row = NB_DEV * N_NARROW
    slot_of = (target.reshape(N_WIDE, per_row) % counts[:, None]).astype(jnp.int32)

    def one_row(pieces):
        entries, rows_of, cols_of, slots_here = pieces
        index = (slots_here[:, None, None] * BS + rows_of[:, :, None]) * BS + cols_of[:, None, :]
        sums = jax.ops.segment_sum(entries.reshape(-1), index.reshape(-1).astype(jnp.int32), num_segments=S_DEV * BS * BS)
        return sums.reshape(S_DEV, BS, BS)

    partial_value = lax.map(one_row, (a_blocks.reshape(N_WIDE, per_row, BS, BS), row_map.reshape(N_WIDE, per_row, BS), col_map.reshape(N_WIDE, per_row, BS), slot_of))
    target_positions = jnp.arange(S_DEV, dtype=jnp.int32)
    is_live = target_positions[None, :] < counts[:, None]
    suffix_total = jnp.cumsum(counts[::-1])[::-1].astype(jnp.int32)
    start = (COARSE - suffix_total).astype(jnp.int32)
    global_index = jnp.where(is_live, start[:, None] + target_positions[None, :], COARSE).astype(jnp.int32).reshape(-1)
    coarse = jnp.zeros((COARSE, BS, BS), jnp.float32).at[global_index].set(partial_value.reshape(COARSE, BS, BS), mode="drop")
    live_weight = jnp.where(is_live, weights.reshape(N_WIDE, S_DEV), 0).astype(jnp.int32).reshape(-1)
    after = (jnp.cumsum(live_weight[::-1])[::-1] - live_weight).astype(jnp.int32)
    work_offset = jnp.zeros((COARSE,), jnp.int32).at[global_index].set(after, mode="drop")
    return coarse, work_offset
```

```python
import functools

import jax
import jax.numpy as jnp
from jax import lax
from jax.experimental import pallas as pl
from jax.experimental.pallas import tpu as pltpu
from jax.sharding import PartitionSpec as P

F32, BF16 = jnp.float32, jnp.bfloat16
NT = (((1,), (1,)), ((), ()))


def split(a):
    hi = a.astype(BF16)
    return hi, (a - hi.astype(F32)).astype(BF16)


def onehot(vec, pos):
    return jnp.where(vec.astype(F32).astype(BF16) == pos, jnp.ones((), BF16), jnp.zeros((), BF16))


def coarsen_body(slot_ref, me_ref, a_ref, row_ref, col_ref, *outs, places, rows):
    i = pl.program_id(0)
    group, n, _ = a_ref.shape

    @pl.when(i == 0)
    def _():
        for o in outs:
            o[...] = jnp.zeros_like(o)

    iota = lax.broadcasted_iota(jnp.int32, (n, n), 0)
    row_pos = ((iota // rows) ^ me_ref[0]) * rows + iota % rows
    row_pos = row_pos.astype(F32).astype(BF16)
    col_pos = iota.astype(F32).astype(BF16)
    for g in range(group):
        r = onehot(row_ref[g : g + 1, :], row_pos)
        c = onehot(col_ref[g : g + 1, :], col_pos)
        y = jnp.dot(
            jnp.concatenate([r, r], 1), jnp.concatenate(split(a_ref[g]), 0), preferred_element_type=F32
        )
        x = lax.dot_general(
            jnp.concatenate(split(y), 1), jnp.concatenate([c, c], 1), NT, preferred_element_type=F32
        )
        s = slot_ref[i * group + g]
        for rel, (k, b) in enumerate(places):
            outs[k][b, s] += x[rel * rows : (rel + 1) * rows]


def coarsen(slot_of, me, a_blocks, row_map, col_map, slots, parts):
    count, n, _ = a_blocks.shape
    rows = n // parts
    stages = parts.bit_length() - 1
    group = max(g for g in range(8, 49, 8) if count % g == 0)
    places, sizes = [], [0] * (stages + 1)
    for rel in range(parts):
        k = stages if rel == 0 else (rel & -rel).bit_length() - 1
        places.append((k, sizes[k]))
        sizes[k] += 1
    return pl.pallas_call(
        functools.partial(coarsen_body, places=places, rows=rows),
        out_shape=[jax.ShapeDtypeStruct((m, slots, rows, n), F32) for m in sizes],
        grid_spec=pltpu.PrefetchScalarGridSpec(
            num_scalar_prefetch=2,
            grid=(count // group,),
            in_specs=[
                pl.BlockSpec((group, n, n), lambda i, s, m: (i, 0, 0)),
                pl.BlockSpec((group, n), lambda i, s, m: (i, 0)),
                pl.BlockSpec((group, n), lambda i, s, m: (i, 0)),
            ],
            out_specs=[pl.BlockSpec((m, slots, rows, n), lambda i, s, m_: (0, 0, 0, 0)) for m in sizes],
        ),
        compiler_params=pltpu.CompilerParams(dimension_semantics=("arbitrary",)),
        cost_estimate=pl.CostEstimate(
            flops=count * 8 * n**3, bytes_accessed=count * n * n * 4, transcendentals=0
        ),
        name="coarsen",
    )(slot_of, me[None], a_blocks, row_map, col_map)


def exchange(x, axis, bit):
    size = lax.axis_size(axis)
    return lax.ppermute(x, axis, [(i, i ^ bit) for i in range(size)])


def local(a_blocks, row_map, col_map, target, counts, weights):
    slots = weights.shape[0]
    parts = lax.axis_size("narrow")
    nwide = lax.axis_size("wide")
    own = lax.axis_index("wide")
    me = lax.axis_index("narrow")
    bits = [1 << k for k in range(nwide.bit_length() - 1)]

    table = jnp.concatenate([counts, weights])[None, :]
    for bit in bits:
        table = jnp.concatenate([table, exchange(table, "wide", bit)], 0)

    slot_of = target % counts[0]
    outs = coarsen(slot_of, me, a_blocks, row_map, col_map, slots, parts)

    owner = own ^ jnp.arange(nwide, dtype=jnp.int32)
    count_of = table[:, 0]
    later = owner[None, :] >= owner[:, None]
    suffix = jnp.sum(jnp.where(later, count_of[None, :], 0), 1)
    start = nwide * slots - suffix
    shift = start[0] % slots
    slot = jnp.arange(slots, dtype=jnp.int32)
    live = slot[None, :] < count_of[:, None]
    place = jnp.where(live, start[:, None] + slot[None, :], -slots).reshape(-1)
    source = jnp.broadcast_to(owner[:, None], (nwide, slots)).reshape(-1)
    weight_of = table[:, 1:].reshape(-1)
    lane, dest = place % slots, place // slots
    at = slot[:, None] == lane[None, :]
    valid = jnp.any(at & (dest == own)[None, :], 1)
    above = place[None, :] > (own * slots + slot)[:, None]
    offset = jnp.where(valid, jnp.sum(jnp.where(above, weight_of[None, :], 0), 1), 0)
    takes, before = [], source
    for bit in bits:
        low = 2 * bit - 1
        after = (source & ~low) | (dest & low)
        moves = (place >= 0) & (after == own) & (before != own)
        takes.append(jnp.any(at & moves[None, :], 1))
        before = after

    outs = [list(o) for o in outs]
    stages = len(outs) - 1
    own_sum = outs[stages][0]
    rels = [[r for r in range(parts) if r and (r & -r) == 1 << k] for k in range(stages)]
    piece = {0: own_sum}
    for k in range(stages):
        for b, rel in enumerate(rels[k]):
            piece[rel] = outs[k][b]
    for k in range(stages):
        for rel in reversed(rels[k]):
            piece[rel ^ (1 << k)] = piece[rel ^ (1 << k)] + exchange(piece[rel], "narrow", 1 << k)
    value = piece[0]

    value = jnp.roll(value, shift, axis=0)
    for bit, take in zip(bits, takes):
        value = jnp.where(take[:, None, None], exchange(value, "wide", bit), value)
    value = jnp.where(valid[:, None, None], value, 0.0)
    return value, offset.astype(jnp.int32)


def solution(mesh):
    return jax.shard_map(
        local,
        mesh=mesh,
        in_specs=(
            P(("wide", "narrow"), None, None),
            P(("wide", "narrow"), None),
            P(("wide", "narrow"), None),
            P(("wide", "narrow")),
            P("wide"),
            P("wide"),
        ),
        out_specs=(P("wide", "narrow", None), P("wide")),
        check_vma=False,
    )
```

```python
import functools

import jax
import jax.numpy as jnp
from jax import lax
from jax.experimental import pallas as pl
from jax.experimental.pallas import tpu as pltpu
from jax.sharding import PartitionSpec as P


F32, BF16 = jnp.float32, jnp.bfloat16
NT = (((1,), (1,)), ((), ()))
GROUP = 32


def split(a):
    hi = a.astype(BF16)
    return hi, (a - hi.astype(F32)).astype(BF16)


def onehot(vec, pos):
    return jnp.where(vec.astype(F32).astype(BF16) == pos, jnp.ones((), BF16), jnp.zeros((), BF16))


def coarsen_body(
    count_ref, weight_hbm, target_hbm, a_hbm, row_hbm, col_hbm, table_out, *refs, group, piece, axis
):
    outs, refs = refs[:-8], refs[-8:]
    weight_ref, target_ref, row_ref, col_ref, a_buf, y_buf, sems, small_sems = refs
    parts = len(outs)
    count, n, _ = a_buf.shape
    rows = n // parts
    chunks, per = count // group, group // piece
    me = lax.axis_index(axis)

    def copy(k):
        at = pl.ds(k * piece, piece)
        return pltpu.make_async_copy(a_hbm.at[at], a_buf.at[at], sems.at[k])

    small = [
        pltpu.make_async_copy(src, dst, small_sems.at[k])
        for k, (src, dst) in enumerate(
            (
                (row_hbm, row_ref),
                (weight_hbm, weight_ref),
                (target_hbm, target_ref),
                (col_hbm, col_ref),
            )
        )
    ]
    small[0].start()
    copy(0).start()
    for c in small[1:]:
        c.start()
    for k in range(1, min(2, chunks) * per):
        copy(k).start()
    for o in outs:
        o[...] = jnp.zeros_like(o)
    iota = lax.broadcasted_iota(jnp.int32, (n, n), 0)
    row_pos = (((iota // rows) ^ me) * rows + iota % rows).astype(F32).astype(BF16)
    col_pos = iota.astype(F32).astype(BF16)

    for c in small:
        c.wait()
    live = count_ref[0]
    lane = lax.broadcasted_iota(jnp.int32, table_out.shape, 1)
    table = jnp.where(lane == 0, live, 0)
    for k in range(weight_ref.shape[0]):
        table = jnp.where(lane == k + 1, weight_ref[k], table)
    table_out[...] = table
    inverse = 65536 // live + 1

    def rows_step(block, row_vec, g):
        r = onehot(row_vec, row_pos)
        y = jnp.dot(
            jnp.concatenate([r, r], 1), jnp.concatenate(split(a_buf[block]), 0), preferred_element_type=F32
        )
        hi, lo = split(y)
        y_buf[g, :, :n] = hi
        y_buf[g, :, n:] = lo

    def cols_step(block, col_vec, g):
        c = onehot(col_vec, col_pos)
        x = lax.dot_general(y_buf[g], jnp.concatenate([c, c], 1), NT, preferred_element_type=F32)
        t = target_ref[block]
        s = t - ((t * inverse) >> 16) * live
        for rel, o in enumerate(outs):
            o[s] += x[rel * rows : (rel + 1) * rows]

    def vectors(ref, i):
        return ref[pl.ds(pl.multiple_of(i * group, 8), group), :]

    first = row_ref[:group, :]
    for g in range(group):
        if g % piece == 0:
            copy(g // piece).wait()
        rows_step(g, first[g : g + 1], g)

    def step(i, carry):
        for k in range(per):
            copy(i * per + k).wait()

        @pl.when(i + 1 < chunks)
        def _():
            for k in range(per):
                copy((i + 1) * per + k).start()

        row_vecs, col_vecs = vectors(row_ref, i), vectors(col_ref, i - 1)
        for g in range(group):
            cols_step((i - 1) * group + g, col_vecs[g : g + 1], g)
            rows_step(i * group + g, row_vecs[g : g + 1], g)
        return carry

    lax.fori_loop(1, chunks, step, 0)
    last = vectors(col_ref, chunks - 1)
    for g in range(group):
        cols_step((chunks - 1) * group + g, last[g : g + 1], g)


def coarsen(counts, weights, target, a_blocks, row_map, col_map, parts, axis):
    args = (weights, target, a_blocks, row_map, col_map)
    slots = weights.shape[0]
    width = pl.cdiv(slots + 1, 128) * 128
    count, n, _ = a_blocks.shape
    rows = n // parts
    piece = 8
    group = max(g for g in range(piece, GROUP + 1, piece) if count % g == 0)
    hbm = pl.BlockSpec(memory_space=pltpu.HBM)
    vmem = pl.BlockSpec(memory_space=pltpu.VMEM)
    return pl.pallas_call(
        functools.partial(coarsen_body, group=group, piece=piece, axis=axis),
        out_shape=[jax.ShapeDtypeStruct((1, width), jnp.int32)]
        + [jax.ShapeDtypeStruct((slots, rows, n), F32) for _ in range(parts)],
        in_specs=[pl.BlockSpec(memory_space=pltpu.SMEM)] + [hbm] * len(args),
        out_specs=[vmem] * (parts + 1),
        scratch_shapes=[
            pltpu.SMEM(weights.shape, jnp.int32),
            pltpu.SMEM(target.shape, jnp.int32),
            pltpu.VMEM(row_map.shape, jnp.int32),
            pltpu.VMEM(col_map.shape, jnp.int32),
            pltpu.VMEM((count, n, n), F32),
            pltpu.VMEM((group, n, 2 * n), BF16),
            pltpu.SemaphoreType.DMA((count // piece,)),
            pltpu.SemaphoreType.DMA((4,)),
        ],
        compiler_params=pltpu.CompilerParams(vmem_limit_bytes=24 << 20),
        cost_estimate=pl.CostEstimate(
            flops=count * 8 * n**3, bytes_accessed=count * n * n * 4, transcendentals=0
        ),
        name="coarsen",
    )(counts, *(pltpu.with_memory_space_constraint(x, pltpu.HBM) for x in args))


def exchange(x, axis, bit):
    size = lax.axis_size(axis)
    return lax.ppermute(x, axis, [(i, i ^ bit) for i in range(size)])


def local(a_blocks, row_map, col_map, target, counts, weights):
    slots = weights.shape[0]
    parts = lax.axis_size("narrow")
    nwide = lax.axis_size("wide")
    own = lax.axis_index("wide")
    bits = [1 << k for k in range(nwide.bit_length() - 1)]
    lane_bits = [1 << k for k in range(slots.bit_length() - 1)]
    assert slots & (slots - 1) == 0 and nwide & (nwide - 1) == 0 and parts & (parts - 1) == 0

    table, *outs = coarsen(counts, weights, target, a_blocks, row_map, col_map, parts, "narrow")

    for bit in bits:
        table = jnp.concatenate([table, exchange(table, "wide", bit)], 0)

    piece = list(outs)
    for k in range(parts.bit_length() - 1):
        for rel in reversed([r for r in range(parts) if r and (r & -r) == 1 << k]):
            other = exchange(piece[rel], "narrow", 1 << k)
            piece[rel ^ (1 << k)] = piece[rel ^ (1 << k)] + other
    value = piece[0]

    count_of = table[:, 0]
    owner = own ^ jnp.arange(nwide, dtype=jnp.int32)
    later = owner[None, :] >= owner[:, None]
    start = nwide * slots - jnp.sum(jnp.where(later, count_of[None, :], 0), 1)
    slot = jnp.arange(slots, dtype=jnp.int32)
    live = slot[None, :] < count_of[:, None]
    origin = (owner[:, None] * slots + slot[None, :]).reshape(-1)
    place = jnp.where(live, start[:, None] + slot[None, :], -1).reshape(-1)
    weight_of = table[:, 1 : slots + 1].reshape(-1)

    def holds(index, device, such):
        here = index[None, :] == (device * slots + slot)[:, None]
        return jnp.any(here & such[None, :], 1)[:, None, None]

    def take(bit, device):
        before = (origin & -bit) | (place & (bit - 1))
        after = (origin & (-2 * bit)) | (place & (2 * bit - 1))
        return holds(after, device, (place >= 0) & (after != before))

    def turned(x, device):
        for bit in lane_bits:
            pairs = x.reshape(slots // (2 * bit), 2, bit, *x.shape[1:])
            x = jnp.where(take(bit, device), jnp.flip(pairs, 1).reshape(x.shape), x)
        return x

    for bit in bits:
        other = exchange(value, "wide", bit)
        if bit == 1:
            value, other = turned(value, own), turned(other, own ^ bit)
        value = jnp.where(take(bit * slots, own), other, value)
    valid = holds(place, own, place >= 0)
    value = jnp.where(valid, value, 0.0)
    above = place[None, :] > (own * slots + slot)[:, None]
    offset = jnp.where(valid[:, 0, 0], jnp.sum(jnp.where(above, weight_of[None, :], 0), 1), 0)
    return value, offset.astype(jnp.int32)


def solution(mesh):
    return jax.shard_map(
        local,
        mesh=mesh,
        in_specs=(
            P(("wide", "narrow"), None, None),
            P(("wide", "narrow"), None),
            P(("wide", "narrow"), None),
            P(("wide", "narrow")),
            P("wide"),
            P("wide"),
        ),
        out_specs=(P("wide", "narrow", None), P("wide")),
        check_vma=False,
    )
```

```python
import functools

import jax
import jax.numpy as jnp
from jax import lax
from jax.experimental import pallas as pl
from jax.experimental.pallas import tpu as pltpu
from jax.sharding import PartitionSpec as P


F32, BF16 = jnp.float32, jnp.bfloat16
NT = (((1,), (1,)), ((), ()))
GROUP = 48


def split(a):
    hi = a.astype(BF16)
    return hi, (a - hi.astype(F32)).astype(BF16)


def onehot(vec, pos):
    return jnp.where(vec.astype(F32).astype(BF16) == pos, jnp.ones((), BF16), jnp.zeros((), BF16))


def coarsen_body(
    count_ref, weight_hbm, target_hbm, a_hbm, row_hbm, col_hbm, table_out, *refs, group, piece, axis
):
    outs, refs = refs[:-8], refs[-8:]
    weight_ref, target_ref, row_ref, col_ref, a_buf, y_buf, sems, small_sems = refs
    parts = len(outs)
    count, n, _ = a_buf.shape
    rows = n // parts
    chunks, per = count // group, group // piece
    me = lax.axis_index(axis)

    def copy(k):
        at = pl.ds(k * piece, piece)
        return pltpu.make_async_copy(a_hbm.at[at], a_buf.at[at], sems.at[k])

    def copy_group(i):
        at = pl.ds(i * group, group)
        return pltpu.make_async_copy(a_hbm.at[at], a_buf.at[at], sems.at[per - 1 + i])

    small = [
        pltpu.make_async_copy(src, dst, small_sems.at[k])
        for k, (src, dst) in enumerate(
            (
                (row_hbm, row_ref),
                (weight_hbm, weight_ref),
                (target_hbm, target_ref),
                (col_hbm, col_ref),
            )
        )
    ]
    small[0].start()
    copy(0).start()
    for c in small[1:]:
        c.start()
    for k in range(1, per):
        copy(k).start()
    if chunks > 1:
        copy_group(1).start()
    for o in outs:
        o[...] = jnp.zeros_like(o)
    iota = lax.broadcasted_iota(jnp.int32, (n, n), 0)
    row_pos = (((iota // rows) ^ me) * rows + iota % rows).astype(F32).astype(BF16)
    col_pos = iota.astype(F32).astype(BF16)

    for c in small:
        c.wait()
    live = count_ref[0]
    lane = lax.broadcasted_iota(jnp.int32, table_out.shape, 1)
    table = jnp.where(lane == 0, live, 0)
    for k in range(weight_ref.shape[0]):
        table = jnp.where(lane == k + 1, weight_ref[k], table)
    table_out[...] = table
    inverse = 65536 // live + 1

    def rows_step(block, row_vec, g):
        r = onehot(row_vec, row_pos)
        y = jnp.dot(
            jnp.concatenate([r, r], 1), jnp.concatenate(split(a_buf[block]), 0), preferred_element_type=F32
        )
        hi, lo = split(y)
        y_buf[g, :, :n] = hi
        y_buf[g, :, n:] = lo

    def cols_step(block, col_vec, g):
        c = onehot(col_vec, col_pos)
        x = lax.dot_general(y_buf[g], jnp.concatenate([c, c], 1), NT, preferred_element_type=F32)
        t = target_ref[block]
        s = t - ((t * inverse) >> 16) * live
        for rel, o in enumerate(outs):
            o[s] += x[rel * rows : (rel + 1) * rows]

    def vectors(ref, i):
        return ref[pl.ds(pl.multiple_of(i * group, 8), group), :]

    first = row_ref[:group, :]
    for g in range(group):
        if g % piece == 0:
            copy(g // piece).wait()
        rows_step(g, first[g : g + 1], g)

    def step(i, carry):
        copy_group(i).wait()

        @pl.when(i + 1 < chunks)
        def _():
            copy_group(i + 1).start()

        row_vecs, col_vecs = vectors(row_ref, i), vectors(col_ref, i - 1)
        for g in range(group):
            cols_step((i - 1) * group + g, col_vecs[g : g + 1], g)
            rows_step(i * group + g, row_vecs[g : g + 1], g)
        return carry

    lax.fori_loop(1, chunks, step, 0)
    last = vectors(col_ref, chunks - 1)
    for g in range(group):
        cols_step((chunks - 1) * group + g, last[g : g + 1], g)


def coarsen(counts, weights, target, a_blocks, row_map, col_map, parts, axis):
    args = (weights, target, a_blocks, row_map, col_map)
    slots = weights.shape[0]
    width = pl.cdiv(slots + 1, 128) * 128
    count, n, _ = a_blocks.shape
    rows = n // parts
    group = max(g for g in range(8, GROUP + 1, 8) if count % g == 0)
    piece = group // 2 if group % 16 == 0 else group
    hbm = pl.BlockSpec(memory_space=pltpu.HBM)
    vmem = pl.BlockSpec(memory_space=pltpu.VMEM)
    return pl.pallas_call(
        functools.partial(coarsen_body, group=group, piece=piece, axis=axis),
        out_shape=[jax.ShapeDtypeStruct((1, width), jnp.int32)]
        + [jax.ShapeDtypeStruct((slots, rows, n), F32) for _ in range(parts)],
        in_specs=[pl.BlockSpec(memory_space=pltpu.SMEM)] + [hbm] * len(args),
        out_specs=[vmem] * (parts + 1),
        scratch_shapes=[
            pltpu.SMEM(weights.shape, jnp.int32),
            pltpu.SMEM(target.shape, jnp.int32),
            pltpu.VMEM(row_map.shape, jnp.int32),
            pltpu.VMEM(col_map.shape, jnp.int32),
            pltpu.VMEM((count, n, n), F32),
            pltpu.VMEM((group, n, 2 * n), BF16),
            pltpu.SemaphoreType.DMA((group // piece + count // group - 1,)),
            pltpu.SemaphoreType.DMA((4,)),
        ],
        compiler_params=pltpu.CompilerParams(vmem_limit_bytes=24 << 20),
        cost_estimate=pl.CostEstimate(
            flops=count * 8 * n**3, bytes_accessed=count * n * n * 4, transcendentals=0
        ),
        name="coarsen",
    )(counts, *(pltpu.with_memory_space_constraint(x, pltpu.HBM) for x in args))


def exchange(x, axis, bit):
    size = lax.axis_size(axis)
    return lax.ppermute(x, axis, [(i, i ^ bit) for i in range(size)])


def local(a_blocks, row_map, col_map, target, counts, weights):
    slots = weights.shape[0]
    parts = lax.axis_size("narrow")
    nwide = lax.axis_size("wide")
    own = lax.axis_index("wide")
    bits = [1 << k for k in range(nwide.bit_length() - 1)]
    lane_bits = [1 << k for k in range(slots.bit_length() - 1)]
    assert slots & (slots - 1) == 0 and nwide & (nwide - 1) == 0 and parts & (parts - 1) == 0

    table, *outs = coarsen(counts, weights, target, a_blocks, row_map, col_map, parts, "narrow")

    for bit in bits:
        table = jnp.concatenate([table, exchange(table, "wide", bit)], 0)

    piece = list(outs)
    for k in range(parts.bit_length() - 1):
        for rel in reversed([r for r in range(parts) if r and (r & -r) == 1 << k]):
            other = exchange(piece[rel], "narrow", 1 << k)
            piece[rel ^ (1 << k)] = piece[rel ^ (1 << k)] + other
    value = piece[0]

    count_of = table[:, 0]
    owner = own ^ jnp.arange(nwide, dtype=jnp.int32)
    later = owner[None, :] >= owner[:, None]
    start = nwide * slots - jnp.sum(jnp.where(later, count_of[None, :], 0), 1)
    slot = jnp.arange(slots, dtype=jnp.int32)
    live = slot[None, :] < count_of[:, None]
    origin = (owner[:, None] * slots + slot[None, :]).reshape(-1)
    place = jnp.where(live, start[:, None] + slot[None, :], -1).reshape(-1)
    weight_of = table[:, 1 : slots + 1].reshape(-1)

    def holds(index, device, such):
        here = index[None, :] == (device * slots + slot)[:, None]
        return jnp.any(here & such[None, :], 1)[:, None, None]

    def take(bit, device):
        before = (origin & -bit) | (place & (bit - 1))
        after = (origin & (-2 * bit)) | (place & (2 * bit - 1))
        return holds(after, device, (place >= 0) & (after != before))

    def turned(x, device):
        for bit in lane_bits:
            pairs = x.reshape(slots // (2 * bit), 2, bit, *x.shape[1:])
            x = jnp.where(take(bit, device), jnp.flip(pairs, 1).reshape(x.shape), x)
        return x

    for bit in bits:
        other = exchange(value, "wide", bit)
        if bit == 1:
            value, other = turned(value, own), turned(other, own ^ bit)
        value = jnp.where(take(bit * slots, own), other, value)
    valid = holds(place, own, place >= 0)
    value = jnp.where(valid, value, 0.0)
    above = place[None, :] > (own * slots + slot)[:, None]
    offset = jnp.where(valid[:, 0, 0], jnp.sum(jnp.where(above, weight_of[None, :], 0), 1), 0)
    return value, offset.astype(jnp.int32)


def solution(mesh):
    return jax.shard_map(
        local,
        mesh=mesh,
        in_specs=(
            P(("wide", "narrow"), None, None),
            P(("wide", "narrow"), None),
            P(("wide", "narrow"), None),
            P(("wide", "narrow")),
            P("wide"),
            P("wide"),
        ),
        out_specs=(P("wide", "narrow", None), P("wide")),
        check_vma=False,
    )
```

```python
import functools

import jax
import jax.numpy as jnp
from jax import lax
from jax.experimental import pallas as pl
from jax.experimental.pallas import tpu as pltpu
from jax.sharding import PartitionSpec as P


F32, BF16 = jnp.float32, jnp.bfloat16
NT = (((1,), (1,)), ((), ()))
GROUP = 48


def split(a):
    hi = a.astype(BF16)
    return hi, (a - hi.astype(F32)).astype(BF16)


def onehot(vec, pos):
    return jnp.where(vec.astype(F32).astype(BF16) == pos, jnp.ones((), BF16), jnp.zeros((), BF16))


def coarsen_body(
    count_ref, weight_hbm, target_hbm, a_hbm, row_hbm, col_hbm, table_out, *refs, group, piece, axis
):
    outs, refs = refs[:-8], refs[-8:]
    weight_ref, target_ref, row_ref, col_ref, a_buf, y_buf, sems, small_sems = refs
    parts = len(outs)
    count, n, _ = a_buf.shape
    rows = n // parts
    chunks, per = count // group, group // piece
    me = lax.axis_index(axis)

    def copy(k):
        at = pl.ds(k * piece, piece)
        return pltpu.make_async_copy(a_hbm.at[at], a_buf.at[at], sems.at[k])

    def copy_group(i):
        at = pl.ds(i * group, group)
        return pltpu.make_async_copy(a_hbm.at[at], a_buf.at[at], sems.at[per - 1 + i])

    small = [
        pltpu.make_async_copy(src, dst, small_sems.at[k])
        for k, (src, dst) in enumerate(
            (
                (row_hbm, row_ref),
                (weight_hbm, weight_ref),
                (target_hbm, target_ref),
                (col_hbm, col_ref),
            )
        )
    ]
    small[0].start()
    copy(0).start()
    for c in small[1:]:
        c.start()
    for k in range(1, per):
        copy(k).start()
    if chunks > 1:
        copy_group(1).start()
    for o in outs:
        o[...] = jnp.zeros_like(o)
    iota = lax.broadcasted_iota(jnp.int32, (n, n), 0)
    row_pos = (((iota // rows) ^ me) * rows + iota % rows).astype(F32).astype(BF16)
    col_pos = iota.astype(F32).astype(BF16)

    for c in small:
        c.wait()
    live = count_ref[0]
    lane = lax.broadcasted_iota(jnp.int32, table_out.shape, 1)
    table = jnp.where(lane == 0, live, 0)
    for k in range(weight_ref.shape[0]):
        table = jnp.where(lane == k + 1, weight_ref[k], table)
    table_out[...] = table
    inverse = 65536 // live + 1

    def rows_step(block, row_vec, g):
        r = onehot(row_vec, row_pos)
        y = jnp.dot(
            jnp.concatenate([r, r], 1), jnp.concatenate(split(a_buf[block]), 0), preferred_element_type=F32
        )
        hi, lo = split(y)
        y_buf[g, :, :n] = hi
        y_buf[g, :, n:] = lo

    def cols_step(block, col_vec, g):
        c = onehot(col_vec, col_pos)
        x = lax.dot_general(y_buf[g], jnp.concatenate([c, c], 1), NT, preferred_element_type=F32)
        t = target_ref[block]
        s = t - ((t * inverse) >> 16) * live
        for rel, o in enumerate(outs):
            o[s] += x[rel * rows : (rel + 1) * rows]

    def vectors(ref, i):
        return ref[pl.ds(pl.multiple_of(i * group, 8), group), :]

    first = row_ref[:group, :]
    for g in range(group):
        if g % piece == 0:
            copy(g // piece).wait()
        rows_step(g, first[g : g + 1], g)

    def step(i, carry):
        copy_group(i).wait()

        @pl.when(i + 1 < chunks)
        def _():
            copy_group(i + 1).start()

        row_vecs, col_vecs = vectors(row_ref, i), vectors(col_ref, i - 1)
        for g in range(group):
            cols_step((i - 1) * group + g, col_vecs[g : g + 1], g)
            rows_step(i * group + g, row_vecs[g : g + 1], g)
        return carry

    lax.fori_loop(1, chunks, step, 0)
    last = vectors(col_ref, chunks - 1)
    for g in range(group):
        cols_step((chunks - 1) * group + g, last[g : g + 1], g)


def coarsen(counts, weights, target, a_blocks, row_map, col_map, parts, axis):
    args = (weights, target, a_blocks, row_map, col_map)
    slots = weights.shape[0]
    width = pl.cdiv(slots + 1, 128) * 128
    count, n, _ = a_blocks.shape
    rows = n // parts
    group = max(g for g in range(8, GROUP + 1, 8) if count % g == 0)
    piece = group // 2 if group % 16 == 0 else group
    hbm = pl.BlockSpec(memory_space=pltpu.HBM)
    vmem = pl.BlockSpec(memory_space=pltpu.VMEM)
    return pl.pallas_call(
        functools.partial(coarsen_body, group=group, piece=piece, axis=axis),
        out_shape=[jax.ShapeDtypeStruct((1, width), jnp.int32)]
        + [jax.ShapeDtypeStruct((slots, rows, n), F32) for _ in range(parts)],
        in_specs=[pl.BlockSpec(memory_space=pltpu.SMEM)] + [hbm] * len(args),
        out_specs=[vmem] * (parts + 1),
        scratch_shapes=[
            pltpu.SMEM(weights.shape, jnp.int32),
            pltpu.SMEM(target.shape, jnp.int32),
            pltpu.VMEM(row_map.shape, jnp.int32),
            pltpu.VMEM(col_map.shape, jnp.int32),
            pltpu.VMEM((count, n, n), F32),
            pltpu.VMEM((group, n, 2 * n), BF16),
            pltpu.SemaphoreType.DMA((group // piece + count // group - 1,)),
            pltpu.SemaphoreType.DMA((4,)),
        ],
        compiler_params=pltpu.CompilerParams(vmem_limit_bytes=24 << 20),
        cost_estimate=pl.CostEstimate(
            flops=count * 8 * n**3, bytes_accessed=count * n * n * 4, transcendentals=0
        ),
        name="coarsen",
    )(counts, *(pltpu.with_memory_space_constraint(x, pltpu.HBM) for x in args))


def exchange(x, axis, bit):
    size = lax.axis_size(axis)
    return lax.ppermute(x, axis, [(i, i ^ bit) for i in range(size)])


def local(a_blocks, row_map, col_map, target, counts, weights):
    slots = weights.shape[0]
    parts = lax.axis_size("narrow")
    nwide = lax.axis_size("wide")
    own = lax.axis_index("wide")
    bits = [1 << k for k in range(nwide.bit_length() - 1)]
    lane_bits = [1 << k for k in range(slots.bit_length() - 1)]
    assert slots & (slots - 1) == 0 and nwide & (nwide - 1) == 0 and parts & (parts - 1) == 0

    table, *outs = coarsen(counts, weights, target, a_blocks, row_map, col_map, parts, "narrow")

    ranks = [0]
    for bit in bits[:1] + bits[:0:-1]:
        ranks += [i ^ bit for i in ranks]
        table = jnp.concatenate([table, exchange(table, "wide", bit)], 0)

    piece = list(outs)
    for k in range(parts.bit_length() - 1):
        for rel in reversed([r for r in range(parts) if r and (r & -r) == 1 << k]):
            other = exchange(piece[rel], "narrow", 1 << k)
            piece[rel ^ (1 << k)] = piece[rel ^ (1 << k)] + other
    value = piece[0]

    count_of = table[:, 0]
    owner = own ^ jnp.array(ranks, jnp.int32)
    later = owner[None, :] >= owner[:, None]
    start = nwide * slots - jnp.sum(jnp.where(later, count_of[None, :], 0), 1)
    slot = jnp.arange(slots, dtype=jnp.int32)
    live = slot[None, :] < count_of[:, None]
    origin = (owner[:, None] * slots + slot[None, :]).reshape(-1)
    place = jnp.where(live, start[:, None] + slot[None, :], -1).reshape(-1)
    weight_of = table[:, 1 : slots + 1].reshape(-1)

    def holds(index, device, such):
        here = index[None, :] == (device * slots + slot)[:, None]
        return jnp.any(here & such[None, :], 1)[:, None, None]

    def take(bit, device):
        before = (origin & -bit) | (place & (bit - 1))
        after = (origin & (-2 * bit)) | (place & (2 * bit - 1))
        return holds(after, device, (place >= 0) & (after != before))

    def turned(x, device):
        for bit in lane_bits:
            pairs = x.reshape(slots // (2 * bit), 2, bit, *x.shape[1:])
            x = jnp.where(take(bit, device), jnp.flip(pairs, 1).reshape(x.shape), x)
        return x

    for bit in bits:
        other = exchange(value, "wide", bit)
        if bit == 1:
            value, other = turned(value, own), turned(other, own ^ bit)
        value = jnp.where(take(bit * slots, own), other, value)
    valid = holds(place, own, place >= 0)
    value = jnp.where(valid, value, 0.0)
    above = place[None, :] > (own * slots + slot)[:, None]
    offset = jnp.where(valid[:, 0, 0], jnp.sum(jnp.where(above, weight_of[None, :], 0), 1), 0)
    return value, offset.astype(jnp.int32)


def solution(mesh):
    return jax.shard_map(
        local,
        mesh=mesh,
        in_specs=(
            P(("wide", "narrow"), None, None),
            P(("wide", "narrow"), None),
            P(("wide", "narrow"), None),
            P(("wide", "narrow")),
            P("wide"),
            P("wide"),
        ),
        out_specs=(P("wide", "narrow", None), P("wide")),
        check_vma=False,
    )
```
